32 devices in a mesh: space: 4 (over y, core), tm: 8 (over z, x).
Axes of the slice: x: 2, y: 2, z: 4, core: 2. Of those that a mesh axis runs over, the one named last changes fastest.
Arguments:
- snapshots: float32 [2048, 30720], P('tm', 'space'), may hold values from -6 to 6
- closing: float32 [128, 30720], P(None, 'space'), may hold values from -6 to 6
- weights: float32 [30720], P('space'), may hold values from 0.25 to 36, as said below
- bin_index: int32 [64], replicated, may hold values from 0 to 128, as said below
Outputs:
- spectra: float32 [64, 2, 16, 16], P('tm', None, 'space')
The draws below stay inside these ranges and needn't reach their ends.
Inputs may be any that keep to these rules, and one draw needn't show every extreme that they name: `bin_index`: distinct bins. Positive weights.
All inputs are finite; a program needn't handle non-finite values.
Results may differ from the reference program's by a relative error of at most 0.0003.
Values sent between devices are 32-bit elements; how exact they have to be, the bound alone decides.
A program may use at most 128 MiB of HBM per device.

```python
import jax
import jax.numpy as jnp
from jax import lax

NFFT = 256
NBINS = 64
P_DEV = 7680
EXTRA = 128
NBLK = 16
NT = 2048
NPTS = 30720
N_SPACE = 4


def draw_weights(key, part):
    position = jnp.arange(NPTS, dtype=jnp.float32) / (NPTS - 1)
    roughness = jnp.exp(jax.random.uniform(key, (NPTS,), jnp.float32, jnp.log(0.5), jnp.log(2.0)))
    return roughness * jnp.exp(jnp.log(3.0) * position)


def draw_bin_index(key, part):
    shuffled = jax.random.permutation(jax.random.fold_in(key, 11), NFFT // 2 + 1)
    return shuffled[:NBINS].astype(jnp.int32)


def level_of(key, dims, shards, smallest, high):
    factor_of = 1.0
    for dim, blocks in shards:
        heights = jax.random.uniform(jax.random.fold_in(jax.random.fold_in(key, 6), dim), (blocks,), jnp.float32, smallest / len(shards), high / len(shards))
        factor_of = factor_of * jnp.repeat(jnp.exp(heights), dims[dim] // blocks).reshape((-1,) + (1,) * (len(dims) - 1 - dim))
    return factor_of


def bell_draw(own_key, dims, deviation, reach, shards=(), kind=jnp.bfloat16):
    array = jax.random.normal(own_key, dims, jnp.float32) * deviation
    if len(shards) > 0:
        array = level_of(own_key, dims, shards, -0.22, 0.18) * array
    return jnp.clip(array, min=-reach, max=reach).astype(kind)


def setup_inputs(seed: int = 0) -> dict:
    key_list = jax.random.split(jax.random.key(seed), 5)
    snapshots = bell_draw(key_list[0], (NT, NPTS), 1.0, 6.0, ((0, 8), (1, 4)), jnp.float32)
    closing = bell_draw(key_list[1], (EXTRA, NPTS), 1.0, 6.0, ((1, 4),), jnp.float32)
    weights = draw_weights(jax.random.fold_in(key_list[4], 71), 0)
    bin_index = draw_bin_index(jax.random.fold_in(key_list[4], 71), 0)
    return {"snapshots": snapshots, "closing": closing, "weights": weights, "bin_index": bin_index}


def spectral_table(bin_index, length):
    sample = jnp.arange(length, dtype=jnp.int32)
    window = 0.5 - 0.5 * jnp.cos(2.0 * jnp.pi * sample.astype(jnp.float32) / length)
    phase_turns = (sample[:, None] * bin_index[None, :]) % length
    phase_angle = 2.0 * jnp.pi * phase_turns.astype(jnp.float32) / length
    paired = jnp.stack([window[:, None] * jnp.cos(phase_angle), -window[:, None] * jnp.sin(phase_angle)], axis=2)
    return paired.reshape(length, 2 * bin_index.shape[0])


def cross_spectra(first_set, second_set):
    products = jnp.einsum("kaip,kbjp->kabij", first_set, second_set, precision=lax.Precision.HIGHEST)
    real_part = products[:, 0, 0] + products[:, 1, 1]
    imag_part = products[:, 0, 1] - products[:, 1, 0]
    return jnp.stack([real_part, imag_part], axis=1)


def reference(snapshots, closing, weights, bin_index):
    basis_table = spectral_table(bin_index, NFFT)
    starts = jnp.arange(NBLK, dtype=jnp.int32) * (NFFT // 2)

    def group_sum(running, group_index):
        column_start = (group_index * P_DEV).astype(jnp.int32)
        columns = lax.dynamic_slice_in_dim(snapshots, column_start, P_DEV, 1)
        series = jnp.concatenate([columns, lax.dynamic_slice_in_dim(closing, column_start, P_DEV, 1)], axis=0)
        weight = lax.dynamic_slice_in_dim(weights, column_start, P_DEV, 0)

        def transform(begin_row):
            window_rows = lax.dynamic_slice_in_dim(series, begin_row, NFFT, 0)
            return lax.dot_general(basis_table, window_rows, (((0,), (0,)), ((), ())), precision=lax.Precision.HIGHEST)

        spectrum = lax.map(transform, starts)
        spectrum = spectrum.reshape(NBLK, NBINS, 2, P_DEV).transpose(1, 2, 0, 3)
        return running + cross_spectra(spectrum, spectrum * weight), None

    zeros_start = jnp.zeros((NBINS, 2, NBLK, NBLK), jnp.float32)
    cross_sum, unused = lax.scan(group_sum, zeros_start, jnp.arange(N_SPACE, dtype=jnp.int32))
    energy = jnp.trace(cross_sum[:, 0], axis1=1, axis2=2)
    return cross_sum * (NBLK / energy)[:, None, None, None]
```

```python
import functools

import jax
import jax.numpy as jnp
import numpy as np
from jax import lax
from jax.experimental import pallas as pl
from jax.experimental.pallas import tpu as pltpu
from jax.sharding import PartitionSpec as P

NFFT = 256
NBINS = 64
LANES = 128
MESH = pl.DeviceIdType.MESH


def passed_along(array, axis, by):
    peers = lax.axis_size(axis)
    pairs = [(i, i + by) for i in range(peers) if 0 <= i + by < peers]
    return lax.ppermute(array, axis, pairs)


def spectral_table(bin_index, length):
    sample = jnp.arange(length, dtype=jnp.int32)
    window = 0.5 - 0.5 * jnp.cos(2.0 * jnp.pi * sample.astype(jnp.float32) / length)
    phase_turns = sample[:, None] * bin_index[None, :] % length
    phase_angle = 2.0 * jnp.pi * phase_turns.astype(jnp.float32) / length
    paired = jnp.stack(
        [window[:, None] * jnp.cos(phase_angle), -window[:, None] * jnp.sin(phase_angle)], axis=2
    )
    return paired.reshape(length, 2 * bin_index.shape[0])


def cross_spectra(first_set, second_set):
    products = jnp.einsum(
        "kaip,kbjp->kabij", first_set, second_set, precision=lax.Precision.HIGHEST
    )
    real_part = products[:, 0, 0] + products[:, 1, 1]
    imag_part = products[:, 0, 1] - products[:, 1, 0]
    return jnp.stack([real_part, imag_part], axis=1)


def body(snapshots, closing, weights, bin_index):
    stride_rows = NFFT // 2
    tail_rows = closing.shape[0]
    blocks_here = snapshots.shape[0] // stride_rows
    points = snapshots.shape[1]
    width_tm = lax.axis_size("tm")
    width_space = lax.axis_size("space")
    blocks_all = blocks_here * width_tm
    own_rows = blocks_all // width_space
    basis_table = spectral_table(bin_index, NFFT)
    incoming = passed_along(snapshots[:tail_rows], "tm", -1)
    last_device = lax.axis_index("tm") == width_tm - 1
    series = jnp.concatenate([snapshots, jnp.where(last_device, closing, incoming)], axis=0)
    leading = series[: blocks_here * stride_rows].reshape(blocks_here, stride_rows, points)
    trailing = series[stride_rows:].reshape(blocks_here, stride_rows, points)
    pieces = jnp.concatenate([leading, trailing], axis=1)
    spectrum = jnp.einsum("nc,bnp->cbp", basis_table, pieces, precision=lax.Precision.HIGHEST)
    spectrum = spectrum.reshape(NBINS, 2, blocks_here, points)
    gathered = lax.all_to_all(spectrum, "tm", split_axis=0, concat_axis=2, tiled=True)
    weighted = gathered * weights
    summed = lax.psum_scatter(
        cross_spectra(gathered, weighted).transpose(2, 0, 1, 3),
        "space",
        scatter_dimension=0,
        tiled=True,
    )
    row_ids = lax.axis_index("space") * own_rows + jnp.arange(own_rows, dtype=jnp.int32)
    diagonal = (row_ids[:, None] == jnp.arange(blocks_all, dtype=jnp.int32)[None, :]).astype(
        jnp.float32
    )
    local_trace = jnp.einsum(
        "rkj,rj->k", summed[:, :, 0, :], diagonal, precision=lax.Precision.HIGHEST
    )
    energy = lax.psum(local_trace, "space")
    spectra = summed * (blocks_all / energy)[None, :, None, None]
    return spectra.transpose(1, 2, 0, 3)


def tile_start(device, tiles, width_tm, space):
    return (device * tiles + (space % 2) * (width_tm // 2)) // width_tm


def halves(value):
    high = value.astype(jnp.bfloat16)
    return high, (value - high.astype(jnp.float32)).astype(jnp.bfloat16)


def matmul(a, b):
    return lax.dot_general(a, b, (((1,), (0,)), ((), ())), preferred_element_type=jnp.float32)


def matmul_nt(a, b):
    return lax.dot_general(a, b, (((1,), (1,)), ((), ())), preferred_element_type=jnp.float32)


def exact(a, b):
    return jnp.dot(a, b, precision=lax.Precision.HIGHEST, preferred_element_type=jnp.float32)


def picked(selector, values):
    high, low = halves(values)
    return matmul(selector, high) + matmul(selector, low)


def picked_right(values, selector):
    high, low = halves(values)
    return matmul(high, selector) + matmul(low, selector)


def table_rows(bins, length):
    shape = (bins.shape[0], length)
    sample = lax.broadcasted_iota(jnp.int32, shape, 1)
    odd = (lax.broadcasted_iota(jnp.int32, shape, 0) & 1) == 1
    window = 0.5 - 0.5 * jnp.cos(2.0 * jnp.pi * sample.astype(jnp.float32) / length)
    turns = (sample * bins) & (length - 1)
    angle = 2.0 * jnp.pi * turns.astype(jnp.float32) / length
    return window * jnp.where(odd, -jnp.sin(angle), jnp.cos(angle))


def kernel(
    n,
    n_space,
    snap_ref,
    closing_ref,
    weights_ref,
    bins_ref,
    left_ref,
    even_ref,
    odd_ref,
    ones_ref,
    out_ref,
    series,
    table_ref,
    a_high,
    a_low,
    b_high,
    b_low,
    gram,
    part,
    rows_in,
    mine,
    spread,
    local_sem,
    send_sem,
    recv_sem,
    part_send,
    part_recv,
    space_send,
    space_recv,
):
    me = lax.axis_index("tm")
    here = lax.axis_index("space")
    rows, points = snap_ref.shape
    tail_rows = closing_ref.shape[0]
    tiles = points // LANES
    slots = series.shape[0]
    hop = NFFT // 2
    blocks_all = n * rows // hop
    channels = bins_ref.shape[0]
    group = channels // n

    near = me // (n // 2) * (n // 2)
    far = n // 2 - near

    def peer_of(k):
        return lax.rem(me + k, n)

    def near_peer(k):
        return near + lax.rem(me - near + k, n // 2)

    def far_peer(k):
        return far + lax.rem(me - near + k, n // 2)

    peers_near = [near_peer(k) for k in range(1, n // 2)]
    peers_far = [far_peer(k) for k in range(n // 2)]

    def begin(device):
        return tile_start(device, tiles, n, here)

    def count(device):
        return begin(device + 1) - begin(device)

    my_start, my_count = begin(me), count(me)

    def columns(tile):
        return pl.ds(pl.multiple_of(tile * LANES, LANES), LANES)

    def own_copies(t):
        return (
            pltpu.make_async_copy(
                snap_ref.at[:, columns(my_start + t)],
                series.at[t, pl.ds(pl.multiple_of(me * rows, rows), rows)],
                local_sem.at[0, t],
            ),
            pltpu.make_async_copy(
                closing_ref.at[:, columns(my_start + t)],
                series.at[t, pl.ds(n * rows, tail_rows)],
                local_sem.at[1, t],
            ),
        )

    def outgoing(t, peer):
        return pltpu.make_async_remote_copy(
            src_ref=snap_ref.at[:, columns(begin(peer) + t)],
            dst_ref=series.at[t, pl.ds(pl.multiple_of(me * rows, rows), rows)],
            send_sem=send_sem.at[t, peer],
            recv_sem=recv_sem.at[t, me],
            device_id={"tm": peer},
            device_id_type=MESH,
        )

    def incoming(t, peer):
        return pltpu.make_async_remote_copy(
            src_ref=snap_ref.at[:, columns(my_start + t)],
            dst_ref=series.at[t, pl.ds(pl.multiple_of(peer * rows, rows), rows)],
            send_sem=send_sem.at[t, peer],
            recv_sem=recv_sem.at[t, peer],
            device_id={"tm": peer},
            device_id_type=MESH,
        )

    barrier = pltpu.get_barrier_semaphore()
    for k in range(1, n):
        pl.semaphore_signal(barrier, inc=1, device_id={"tm": peer_of(k)}, device_id_type=MESH)
    for k in range(1, n_space):
        pl.semaphore_signal(
            barrier, inc=1, device_id={"space": lax.rem(here + k, n_space)}, device_id_type=MESH
        )
    pl.semaphore_wait(barrier, n - 1 + n_space - 1)

    @pl.loop(0, slots)
    def _(t):
        for peer in [peer_of(k) for k in range(1, n)]:

            @pl.when(t < count(peer))
            def _(peer=peer):
                outgoing(t, peer).start()

        @pl.when(t < my_count)
        def _():
            for copy in own_copies(t):
                copy.start()

    @pl.when(my_count < slots)
    def _():
        series[slots - 1] = jnp.zeros(series.shape[1:], jnp.float32)

    gram[...] = jnp.zeros(gram.shape, jnp.float32)
    table_high, table_low = halves(table_rows(bins_ref[...], NFFT))
    table_ref[:channels] = table_high
    table_ref[channels:] = table_low

    @pl.loop(0, slots // 2)
    def _(step):
        def arrived(peers, own):
            for half in range(2):
                t = 2 * step + half

                @pl.when(t < my_count)
                def _(t=t):
                    if own:
                        for copy in own_copies(t):
                            copy.wait()
                    for peer in peers:
                        incoming(t, peer).wait_recv()

        weight = []
        for half in range(2):
            t = 2 * step + half
            held = weights_ref[pl.ds(jnp.minimum(my_start + t, tiles - 1), 1), :]
            weight.append(held * (t < my_count).astype(jnp.float32))
        weight = jnp.concatenate(weight, axis=1)

        def transform(turn, carry):
            block = lax.rem(near * (rows // hop) + turn, blocks_all)
            window = pl.ds(pl.multiple_of(block * hop, hop), NFFT)
            piece = jnp.concatenate(
                [series[2 * step, window, :], series[2 * step + 1, window, :]], axis=1
            )
            high, low = halves(piece)
            both = matmul(table_ref[...], high)
            coef = both[:channels] + both[channels:] + matmul(table_ref[:channels], low)
            first_high, first_low = halves(coef)
            second_high, second_low = halves(coef * weight)
            place = pl.ds(pl.multiple_of(block * group, group), group)
            for g in range(n):
                cut = slice(g * group, (g + 1) * group)
                a_high[g, place, :] = first_high[cut]
                a_low[g, place, :] = first_low[cut]
                b_high[g, place, :] = second_high[cut]
                b_low[g, place, :] = second_low[cut]
            return carry

        ready = blocks_all // 2 - 1
        arrived(peers_near, True)
        lax.fori_loop(0, ready, transform, 0, unroll=ready)
        arrived(peers_far, False)
        lax.fori_loop(ready, blocks_all, transform, 0, unroll=3)

        def products(g, carry):
            gram[g] += (
                matmul_nt(b_high[g], a_high[g])
                + matmul_nt(b_high[g], a_low[g])
                + matmul_nt(b_low[g], a_high[g])
            )
            return carry

        lax.fori_loop(0, n, products, 0, unroll=2)

    size = gram.shape[1]
    row = lax.broadcasted_iota(jnp.int32, (size, size), 0)
    col = lax.broadcasted_iota(jnp.int32, (size, size), 1)
    same_bin = ((row & (group - 1)) >> 1) == ((col & (group - 1)) >> 1)

    def folded(g):
        kept = picked(left_ref[...], jnp.where(same_bin, gram[g], 0.0))
        middle = kept.shape[0] // 2
        return picked_right(kept[:middle], even_ref[...]) + picked_right(
            kept[middle:], odd_ref[...]
        )

    def part_copy(k):
        peer = peer_of(k)
        return pltpu.make_async_remote_copy(
            src_ref=part.at[peer],
            dst_ref=rows_in.at[me],
            send_sem=part_send.at[peer],
            recv_sem=part_recv.at[me],
            device_id={"tm": peer},
            device_id_type=MESH,
        )

    def part_arrival(k):
        peer = peer_of(k)
        return pltpu.make_async_remote_copy(
            src_ref=part.at[peer],
            dst_ref=rows_in.at[peer],
            send_sem=part_send.at[peer],
            recv_sem=part_recv.at[peer],
            device_id={"tm": peer},
            device_id_type=MESH,
        )

    for k in range(1, n):
        part[peer_of(k)] = folded(peer_of(k))
        part_copy(k).start()
    rows_in[me] = folded(me)
    for k in range(1, n):
        part_arrival(k).wait_recv()
    total = rows_in[0]
    for p in range(1, n):
        total = total + rows_in[p]
    mine[...] = total
    spread[here] = total

    def space_copy(k):
        peer = lax.rem(here + k, n_space)
        return pltpu.make_async_remote_copy(
            src_ref=mine,
            dst_ref=spread.at[here],
            send_sem=space_send.at[peer],
            recv_sem=space_recv.at[here],
            device_id={"space": peer},
            device_id_type=MESH,
        )

    def space_arrival(k):
        peer = lax.rem(here + k, n_space)
        return pltpu.make_async_remote_copy(
            src_ref=mine,
            dst_ref=spread.at[peer],
            send_sem=space_send.at[peer],
            recv_sem=space_recv.at[peer],
            device_id={"space": peer},
            device_id_type=MESH,
        )

    for k in range(1, n_space):
        space_copy(k).start()
    for k in range(1, n_space):
        space_arrival(k).wait_recv()
    total = spread[0]
    for p in range(1, n_space):
        total = total + spread[p]
    line = lax.broadcasted_iota(jnp.int32, total.shape, 0)
    lane = lax.broadcasted_iota(jnp.int32, total.shape, 1)
    diagonal = jnp.where(line == (lane & (blocks_all - 1)), total, 0.0)
    trace = jnp.sum(diagonal, axis=0, keepdims=True)
    energy = exact(jnp.broadcast_to(trace, (8, trace.shape[1])), ones_ref[...])[:1]
    out_ref[...] = total * (blocks_all / energy)

    @pl.loop(0, slots)
    def _(t):
        for k in range(1, n):
            peer = peer_of(k)

            @pl.when(t < count(peer))
            def _():
                outgoing(t, peer).wait_send()

    for k in range(1, n):
        part_copy(k).wait_send()
    for k in range(1, n_space):
        space_copy(k).wait_send()


def selections(blocks, group):
    size, bins = blocks * group, group // 2
    block, channel = np.divmod(np.arange(size), group)
    part, second = np.divmod(np.arange(2 * blocks), blocks)
    match = second[:, None] == block[None, :]
    first_half = match & (channel[None, :] % 2 == part[:, None])
    second_half = match & (channel[None, :] % 2 == 1 - part[:, None])
    sign = np.where(part[:, None] == 0, 1.0, -1.0)
    left = np.concatenate([first_half * 1.0, second_half * sign], axis=0)
    bin_of, first = np.divmod(np.arange(bins * blocks), blocks)
    place = (block[:, None] == first[None, :]) & (channel[:, None] // 2 == bin_of[None, :])
    even = place & (channel[:, None] % 2 == 0)
    odd = place & (channel[:, None] % 2 == 1)
    ones = bin_of[:, None] == bin_of[None, :]
    return [jnp.asarray(m, jnp.bfloat16) for m in (left, even, odd)] + [
        jnp.asarray(ones, jnp.float32)
    ]


def fused_body(snapshots, closing, weights, bin_index):
    n, n_space = lax.axis_size("tm"), lax.axis_size("space")
    rows, points = snapshots.shape
    tail_rows = closing.shape[0]
    tiles = points // LANES
    slots = -(-tiles // n)
    blocks_all = n * rows // (NFFT // 2)
    channels = 2 * NBINS
    group = channels // n
    size = blocks_all * group
    shape = (2 * blocks_all, size // 2)
    whole = pl.BlockSpec(memory_space=pltpu.VMEM)
    spread = pl.pallas_call(
        functools.partial(kernel, n, n_space),
        out_shape=jax.ShapeDtypeStruct(shape, jnp.float32),
        in_specs=[pl.BlockSpec(memory_space=pl.ANY)] * 2 + [whole] * 6,
        out_specs=whole,
        scratch_shapes=[
            pltpu.VMEM((slots, n * rows + tail_rows, LANES), jnp.float32),
            pltpu.VMEM((2 * channels, NFFT), jnp.bfloat16),
        ]
        + [pltpu.VMEM((n, size, 2 * LANES), jnp.bfloat16)] * 4
        + [
            pltpu.VMEM((n, size, size), jnp.float32),
            pltpu.VMEM((n,) + shape, jnp.float32),
            pltpu.VMEM((n,) + shape, jnp.float32),
            pltpu.VMEM(shape, jnp.float32),
            pltpu.VMEM((n_space,) + shape, jnp.float32),
            pltpu.SemaphoreType.DMA((2, slots)),
            pltpu.SemaphoreType.DMA((slots, n)),
            pltpu.SemaphoreType.DMA((slots, n)),
            pltpu.SemaphoreType.DMA((n,)),
            pltpu.SemaphoreType.DMA((n,)),
            pltpu.SemaphoreType.DMA((n_space,)),
            pltpu.SemaphoreType.DMA((n_space,)),
        ],
        compiler_params=pltpu.CompilerParams(collective_id=0, has_side_effects=True),
    )(
        snapshots,
        closing,
        weights.reshape(tiles, LANES),
        jnp.repeat(bin_index, 2)[:, None],
        *selections(blocks_all, group),
    )
    by_pair = spread.reshape(2, blocks_all, group // 2, blocks_all).transpose(2, 0, 3, 1)
    own_rows = blocks_all // n_space
    return lax.dynamic_slice_in_dim(by_pair, lax.axis_index("space") * own_rows, own_rows, 2)


def chosen_body(snapshots, closing, weights, bin_index):
    n = lax.axis_size("tm")
    rows, points = snapshots.shape
    group = 2 * NBINS // n
    blocks_all = n * rows // (NFFT // 2)
    slots = -(-(points // LANES) // n)
    fits = (
        2 * NBINS % n == 0
        and n % 2 == 0
        and points % LANES == 0
        and slots % 2 == 0
        and closing.shape[0] == NFFT // 2
        and group == 16
        and blocks_all == 16
    )
    return (fused_body if fits else body)(snapshots, closing, weights, bin_index)


def solution(mesh):
    return jax.shard_map(
        chosen_body,
        mesh=mesh,
        in_specs=(P("tm", "space"), P(None, "space"), P("space"), P()),
        out_specs=P("tm", None, "space", None),
        check_vma=False,
    )
```
